32 devices in a mesh: groups: 2 (over y), chain: 4 (over z), samp: 4 (over x, core).
Axes of the slice: x: 2, y: 2, z: 4, core: 2. Of those that a mesh axis runs over, the one named last changes fastest.
Arguments:
- dosage: bfloat16 [16384, 4096], P('samp', ('groups', 'chain')), parts along dimension 1
- filter_mask: int32 [4096], P(('groups', 'chain')), parts along dimension 0, may hold values 0 or 1
- counts: int32 [8], P(('groups', 'chain')), parts along dimension 0, may hold values from 128 to 512, as said below
Outputs:
- ld_tiles: float32 [8, 512, 3, 512], P(('groups', 'chain'), 'samp'), parts along dimension 0
The draws below stay inside these ranges and needn't reach their ends.
There are 2 independent parts, one for each index of `groups`. The reference program is written for one: setup_inputs(seed, part) draws one part's arguments, and reference() takes and returns one part's arrays. A program takes and returns all parts, laid end to end along the dimension named above; each array names one. Nothing has to cross between parts.
Inputs may be any that keep to these rules, and one draw needn't show every extreme that they name: `counts`: every block but the last holds 512 live variants; the last holds from 128 to 512.
All inputs are finite; a program needn't handle non-finite values. No bound on the sum of `filter_mask` on one device may be relied on, other than what follows from the above.
Results may differ from the reference program's by a relative error of at most 0.0013.
Values may be sent and summed in bfloat16 or wider, within the bound.
No kernel may reach another device: no remote copies, remote signals or barrier semaphores. Data moves between devices by JAX's collectives and lax.ppermute only.
A program may use at most 64 MiB of HBM per device.

```python
import jax
import jax.numpy as jnp
from jax import lax

BLK = 512
BAND = 3
BLOCKS = 4
VARIANTS = 2048
SAMPLES = 16384


def draw_dosage(key, part):
    keys = jax.random.split(jax.random.fold_in(key, 11), 4)
    place = jnp.arange(SAMPLES, dtype=jnp.float32) / SAMPLES
    row_scale = jnp.exp(jnp.log(10.0) * (0.5 * place + 0.5 * jax.random.uniform(keys[0], (SAMPLES,))))
    col_scale = jnp.exp(jnp.log(10.0) * jax.random.uniform(keys[1], (VARIANTS,)))
    centre = jax.random.uniform(keys[2], (VARIANTS,), minval=0.0, maxval=2.0)
    noise = jax.random.normal(keys[3], (SAMPLES, VARIANTS))
    mixed = noise + 0.6 * jnp.roll(noise, 1, axis=1) + 0.3 * jnp.roll(noise, 2, axis=1)
    values = centre[None, :] + 0.3 * mixed * row_scale[:, None] * col_scale[None, :]
    return values.astype(jnp.bfloat16)


def draw_counts(key, part):
    last = jax.random.randint(jax.random.fold_in(key, 23), (), BLK // 4, BLK + 1)
    index = jnp.arange(BLOCKS, dtype=jnp.int32)
    return jnp.where(index == BLOCKS - 1, last, BLK).astype(jnp.int32)


def with_ends(result, key, least, top_value):
    longest = result.shape.index(max(result.shape))
    spots = []
    for shift in (0, 1):
        where = [jax.random.randint(jax.random.fold_in(key, axis), (), 0, length) for axis, length in enumerate(result.shape)]
        where[longest] = (where[longest] + shift) % result.shape[longest]
        spots.append(tuple(where))
    return result.at[spots[0]].set(least).at[spots[1]].set(top_value)


def setup_inputs(seed: int = 0, part: int = 0) -> dict:
    arg_keys = jax.random.split(jax.random.key(seed), 4)
    own_keys = jax.random.split(jax.random.fold_in(arg_keys[3], part), 4)
    return {
        "dosage": draw_dosage(jax.random.fold_in(jax.random.fold_in(arg_keys[3], part), 71), part),
        "filter_mask": with_ends((jax.random.randint(own_keys[1], (VARIANTS,), 0, 8) < 7).astype(jnp.int32), jax.random.fold_in(own_keys[1], 1), 0, 1),
        "counts": draw_counts(jax.random.fold_in(jax.random.fold_in(arg_keys[3], part), 71), part),
    }


def reference(dosage, filter_mask, counts):
    samples = dosage.shape[0]
    values = dosage.astype(jnp.float32)
    mean = lax.optimization_barrier(jnp.sum(values, 0)) / samples
    var = lax.optimization_barrier(jnp.sum(values * values, 0)) / samples - mean * mean
    index = jnp.arange(VARIANTS, dtype=jnp.int32)
    inside = index % BLK
    owner = index // BLK
    live = (inside < counts[owner]).astype(jnp.float32)
    keep = filter_mask.astype(jnp.float32) * live
    scaled = ((values - mean) * lax.rsqrt(var + 1e-05) * keep).astype(jnp.bfloat16)
    padded = jnp.concatenate([scaled, jnp.zeros((samples, 2 * BLK), jnp.bfloat16)], axis=1)

    def one_block(block):
        start = (block * BLK).astype(jnp.int32)
        window = lax.dynamic_slice_in_dim(padded, start, BAND * BLK, 1)
        left = window[:, :BLK]
        tile = lax.dot_general(left, window, (((0,), (0,)), ((), ())), preferred_element_type=jnp.float32)
        return (tile / samples).reshape(BLK, BAND, BLK)
    return lax.map(one_block, jnp.arange(BLOCKS, dtype=jnp.int32))
```

```python
import jax
import jax.numpy as jnp
from jax import lax
from jax.sharding import PartitionSpec as P


LANES = 128


def edges(devices, first):
    pairs = []
    for low in range(first, devices - 1, 2):
        pairs += [(low, low + 1), (low + 1, low)]
    return pairs


def exchange(array, devices, first):
    pairs = edges(devices, first)
    if not pairs:
        return jnp.zeros_like(array)
    return lax.ppermute(array, "chain", pairs)


def partner(devices, me, step):
    if devices & (devices - 1) == 0:
        return me ^ step, [(i, i ^ step) for i in range(devices)]
    return (me + step) % devices, [(i, (i + step) % devices) for i in range(devices)]


def scatter_sum(parts, me, devices):
    own = lax.dynamic_index_in_dim(parts, me, 0, False)
    for step in range(1, devices):
        target, pairs = partner(devices, me, step)
        own = own + lax.ppermute(lax.dynamic_index_in_dim(parts, target, 0, False), "samp", pairs)
    return own


def dot(left, right):
    return lax.dot_general(left, right, (((0,), (0,)), ((), ())), preferred_element_type=jnp.float32)


def standardize(values, mean, scale):
    return ((values.astype(jnp.float32) - mean) * scale).astype(jnp.bfloat16)


def body(dosage, filter_mask, counts):
    chain, samp = lax.axis_size("chain"), lax.axis_size("samp")
    me, block = lax.axis_index("samp"), lax.axis_index("chain")
    even = block % 2 == 0
    local_rows, width = dosage.shape
    samples = local_rows * samp
    step = LANES if width % LANES == 0 else width
    starts = list(range(0, width, step))
    part = width // samp

    raw = []
    for c in starts:
        piece = dosage[:, c : c + step]
        a = exchange(piece, chain, 0)
        b = exchange(piece, chain, 1)
        raw.append((a, b))

    values = dosage.astype(jnp.float32)
    totals, squares = lax.psum((jnp.sum(values, 0), jnp.sum(values * values, 0)), "samp")
    mean = totals / samples
    var = squares / samples - mean * mean
    live = (jnp.arange(width, dtype=jnp.int32) < counts[0]).astype(jnp.float32)
    keep = filter_mask.astype(jnp.float32) * live
    stats = jnp.stack([mean, lax.rsqrt(var + 1e-05) * keep])
    sa = exchange(stats, chain, 0)
    sb = exchange(stats, chain, 1)
    after = jnp.where(even, sa, sb)
    before = jnp.where(even, sb, sa)

    own = standardize(dosage, stats[0], stats[1])
    tile = scatter_sum(dot(own, own).reshape(samp, part, width), me, samp)
    near, far = [], []
    befores, afters = [], []
    for j, c in enumerate(starts):
        a, b = raw[j]
        cols = slice(c, c + step)
        afters.append(standardize(jnp.where(even, a, b), after[0, cols], after[1, cols]))
        befores.append(standardize(jnp.where(even, b, a), before[0, cols], before[1, cols]))
        piece = dot(own, afters[j])
        near.append(scatter_sum(piece.reshape(samp, part, step), me, samp))
    after_all = jnp.concatenate(afters, 1)
    before_all = jnp.concatenate(befores, 1)
    for j, c in enumerate(starts):
        piece = dot(before_all, afters[j])
        far.append(scatter_sum(piece.reshape(samp, part, step), me, samp))
    far = jnp.concatenate(far, 1)
    far = lax.ppermute(far, "chain", [(i + 1, i) for i in range(chain - 1)])
    out = jnp.stack([tile, jnp.concatenate(near, 1), far], 1) / samples
    return out[None]


def solution(mesh):
    in_specs = (P("samp", ("groups", "chain")), P(("groups", "chain")), P(("groups", "chain")))
    out_specs = P(("groups", "chain"), "samp", None, None)
    return jax.shard_map(body, mesh=mesh, in_specs=in_specs, out_specs=out_specs, check_vma=False)
```

```python
import functools

import jax
import jax.numpy as jnp
from jax import lax
from jax.experimental import pallas as pl
from jax.experimental.pallas import tpu as pltpu
from jax.sharding import PartitionSpec as P


LANES = 128
DEPTH = 1024


def exchange(array, devices, first):
    pairs = []
    for low in range(first, devices - 1, 2):
        pairs += [(low, low + 1), (low + 1, low)]
    return lax.ppermute(array, "chain", pairs) if pairs else jnp.zeros_like(array)


def matmul(left, right):
    return lax.dot_general(left, right, (((1,), (0,)), ((), ())), preferred_element_type=jnp.float32)


def accumulate(total, terms):
    return terms if total is None else [t + u for t, u in zip(total, terms)]


def by_distance(parts, me):
    bit = 1
    while bit < len(parts):
        swap = (me // bit) % 2 == 1
        parts = [jnp.where(swap, parts[t ^ bit], parts[t]) for t in range(len(parts))]
        bit *= 2
    return parts


def own_kernel(samp, place_ref, values_ref, mean_ref, scale_ref, own_ref, *outs):
    rows, width = values_ref.shape
    part = width // samp
    total = None
    for k in range(0, rows, DEPTH):
        span = pl.ds(k, DEPTH)
        z = ((values_ref[span, :].astype(jnp.float32) - mean_ref[...]) * scale_ref[...]).astype(jnp.bfloat16)
        flat = z.T
        own_ref[:, span] = flat
        total = accumulate(total, [matmul(flat, z)])
    parts = [total[0][t * part : (t + 1) * part] for t in range(samp)]
    for out_ref, value in zip(outs, by_distance(parts, place_ref[1])):
        out_ref[...] = value


def step_kernel(samp, j, results, place_ref, sa_ref, sb_ref, a_ref, b_ref, own_ref, *rest):
    nears, fars = rest[:j], rest[j : 2 * j]
    saved, outs = rest[2 * j : len(rest) - results], rest[len(rest) - results :]
    rows, step = a_ref.shape
    part, share = own_ref.shape[0] // samp, step // samp
    even, me = place_ref[0] != 0, place_ref[1]
    cols = pl.ds(j * step, step)
    sa, sb = sa_ref[:, cols], sb_ref[:, cols]
    after = jnp.where(even, sa, sb)
    before = jnp.where(even, sb, sa)
    total = None
    for k in range(0, rows, DEPTH):
        span = pl.ds(k, DEPTH)
        a, b = a_ref[span, :].astype(jnp.float32), b_ref[span, :].astype(jnp.float32)
        near = ((jnp.where(even, a, b) - after[0:1]) * after[1:2]).astype(jnp.bfloat16)
        far = ((jnp.where(even, b, a) - before[2:3]) * before[3:4]).astype(jnp.bfloat16).T
        if saved:
            saved[0][span, :] = near
            saved[1][:, span] = far
        terms = [matmul(own_ref[:, span], near)]
        terms += [matmul(fars[i][:, span], near) for i in range(j)]
        terms += [matmul(far, jnp.concatenate([near] + [nears[i][span, :] for i in range(j)], 1))]
        total = accumulate(total, terms)
    blocks = total[1:-1] + [total[-1][:, i * step : (i + 1) * step] for i in range(j + 1)]
    parts = [
        [total[0][t * part : (t + 1) * part]] + [block[t * share : (t + 1) * share] for block in blocks]
        for t in range(samp)
    ]
    parts = [by_distance([parts[t][n] for t in range(samp)], me) for n in range(len(blocks) + 1)]
    if len(outs) != samp:
        outs = [outs[d % 2].at[d // 2] for d in range(samp)]
    for d, out_ref in enumerate(outs):
        row = 0
        for piece in parts:
            size = piece[d].shape[0]
            out_ref[row : row + size, :] = piece[d]
            row += size


def call(kernel, out_shapes, flops, *args):
    vmem = pl.BlockSpec(memory_space=pltpu.VMEM)
    moved = sum(x.size * x.dtype.itemsize for x in args[1:]) + sum(x.size * x.dtype.itemsize for x in out_shapes)
    return pl.pallas_call(
        kernel,
        out_shape=out_shapes,
        in_specs=[pl.BlockSpec(memory_space=pltpu.SMEM)] + [vmem] * (len(args) - 1),
        out_specs=[vmem] * len(out_shapes),
        cost_estimate=pl.CostEstimate(flops=flops, bytes_accessed=moved, transcendentals=0),
        compiler_params=pltpu.CompilerParams(vmem_limit_bytes=VMEM_LIMIT),
    )(*args)


VMEM_LIMIT = 32 * 2**20


def body(dosage, filter_mask, counts):
    chain, samp = lax.axis_size("chain"), lax.axis_size("samp")
    me, block = lax.axis_index("samp"), lax.axis_index("chain")
    even = block % 2 == 0
    place = jnp.stack([even.astype(jnp.int32), me.astype(jnp.int32)])
    local_rows, width = dosage.shape
    samples = local_rows * samp
    step = LANES
    chunks = width // step
    part = width // samp
    share = step // samp

    def spread(vector):
        lead = vector.shape[:-1]
        grid = vector.reshape(*lead, samp, chunks, share)
        return jnp.swapaxes(grid, -3, -2).reshape(*lead, width)

    def payload(j, up):
        lane = jnp.arange(step, dtype=jnp.int32)
        upward = lane // share * part + j * share + lane % share
        source = jnp.where(up, upward, j * step + lane)
        chosen = jnp.arange(width, dtype=jnp.int32)[:, None] == source[None, :]
        return jnp.dot(dosage, chosen.astype(jnp.bfloat16), preferred_element_type=jnp.float32).astype(jnp.bfloat16)

    def scatter_sum(parts):
        total = parts[0]
        for d in range(1, samp):
            total = total + lax.ppermute(parts[d], "samp", [(i, i ^ d) for i in range(samp)])
        return total

    def f32(*shape):
        return jax.ShapeDtypeStruct(shape, jnp.float32)

    def bf16(*shape):
        return jax.ShapeDtypeStruct(shape, jnp.bfloat16)

    raw = []
    for j in range(chunks):
        a = exchange(payload(j, even), chain, 0)
        b = exchange(payload(j, ~even), chain, 1)
        raw.append((a, b))

    values = dosage.astype(jnp.float32)
    totals, squares = lax.psum((jnp.sum(values, 0), jnp.sum(values * values, 0)), "samp")
    mean = totals / samples
    var = squares / samples - mean * mean
    live = (jnp.arange(width, dtype=jnp.int32) < counts[0]).astype(jnp.float32)
    keep = filter_mask.astype(jnp.float32) * live
    scale = lax.rsqrt(var + 1e-05) * keep
    stats = jnp.stack([mean, scale])
    stats = jnp.concatenate([stats, spread(stats)])
    sa = exchange(stats, chain, 0)
    sb = exchange(stats, chain, 1)

    own, *parts = call(
        functools.partial(own_kernel, samp),
        [bf16(width, local_rows)] + [f32(part, width)] * samp,
        2 * local_rows * width * width,
        place, dosage, mean[None], scale[None],
    )
    tile = scatter_sum(parts)

    nears, fars, near_done, shipped = [], [], [], []
    far_done = {}
    for j in range(chunks):
        size = part + (2 * j + 1) * share
        last = j == chunks - 1
        results = [f32(samp // 2, size, step)] * 2 if last else [f32(size, step)] * samp
        saved = [] if last else [bf16(local_rows, step), bf16(step, local_rows)]
        *kept, = call(
            functools.partial(step_kernel, samp, j, len(results)),
            saved + results,
            2 * local_rows * step * (width + (2 * j + 1) * step),
            place, sa, sb, *raw[j], own, *nears, *fars,
        )
        parts = kept[len(saved) :]
        nears += kept[:1] if saved else []
        fars += kept[1:2] if saved else []
        names = [(i, j) for i in range(j)] + [(j, j)] + [(j, i) for i in range(j)]
        for at, name in enumerate(names):
            far_done[name] = (j, at)
        if not last:
            total = scatter_sum(parts)
            near_done.append(total[:part])
            shipped.append(total[part:])
            if j == chunks - 2:
                early = lax.ppermute(
                    jnp.concatenate(shipped), "chain", [(i + 1, i) for i in range(chain - 1)]
                )
        else:
            pair = 2
            kept = parts[0] + lax.ppermute(parts[1], "samp", [(i, i ^ 1) for i in range(samp)])
            near_total, far_total = kept[0][:part], 0.0
            for n in range(samp // pair):
                out = kept[n]
                moved = [i ^ (n * pair) for i in range(samp)]
                pairs = [((c + 1) * samp + i, c * samp + moved[i]) for c in range(chain - 1) for i in range(samp)]
                far_total = far_total + lax.ppermute(out[part:], ("chain", "samp"), pairs)
                if n:
                    near_total = near_total + lax.ppermute(out[:part], "samp", [(i, moved[i]) for i in range(samp)])
            near_done.append(near_total)
    starts, row = [], 0
    for piece in shipped:
        starts.append(row)
        row += piece.shape[0]

    def far_block(i, j):
        at, place = far_done[i, j]
        if at == chunks - 1:
            return far_total[place * share : (place + 1) * share]
        return early[starts[at] + place * share : starts[at] + (place + 1) * share]

    far = jnp.concatenate(
        [jnp.concatenate([far_block(i, j) for j in range(chunks)], 1) for i in range(chunks)], 0
    )
    out = jnp.stack([tile, jnp.concatenate(near_done, 1), far], 1) / samples
    return out[None]


def solution(mesh):
    in_specs = (P("samp", ("groups", "chain")), P(("groups", "chain")), P(("groups", "chain")))
    out_specs = P(("groups", "chain"), "samp", None, None)
    return jax.shard_map(body, mesh=mesh, in_specs=in_specs, out_specs=out_specs, check_vma=False)
```

```python
import functools

import jax
import jax.numpy as jnp
from jax import lax
from jax.experimental import pallas as pl
from jax.experimental.pallas import tpu as pltpu
from jax.sharding import PartitionSpec as P


LANES = 128
DEPTH = 1024
BLOCKS = 8


def exchange(array, devices, first):
    pairs = []
    for low in range(first, devices - 1, 2):
        pairs += [(low, low + 1), (low + 1, low)]
    return lax.ppermute(array, "chain", pairs) if pairs else jnp.zeros_like(array)


def matmul(left, right):
    return lax.dot_general(left, right, (((1,), (0,)), ((), ())), preferred_element_type=jnp.float32)


def accumulate(total, terms):
    return terms if total is None else [t + u for t, u in zip(total, terms)]


def by_distance(parts, me):
    bit = 1
    while bit < len(parts):
        swap = (me // bit) % 2 == 1
        parts = [jnp.where(swap, parts[t ^ bit], parts[t]) for t in range(len(parts))]
        bit *= 2
    return parts


def choose(width, samp, j, even):
    step = LANES
    part, share = width // samp, step // samp
    lane = lax.broadcasted_iota(jnp.int32, (width, step), 1)
    row = lax.broadcasted_iota(jnp.int32, (width, step), 0)
    up = lane // share * part + j * share + lane % share
    down = j * step + lane
    first, second = jnp.where(even, up, down), jnp.where(even, down, up)
    return jnp.concatenate([row == first, row == second], 1).astype(jnp.float32).astype(jnp.bfloat16)


def front_kernel(samp, place_ref, values_hbm, a_hbm, b_hbm, values_ref, a_ref, b_ref, sems):
    rows, width = values_ref.shape
    blocks = sems.shape[1]
    size = rows // blocks
    spans = [pl.ds(k * size, size) for k in range(blocks)]
    arrive = [pltpu.make_async_copy(values_hbm.at[s], values_ref.at[s], sems.at[0, k]) for k, s in enumerate(spans)]
    leave = [pltpu.make_async_copy(a_ref.at[s], a_hbm.at[s], sems.at[1, k]) for k, s in enumerate(spans)]
    leave += [pltpu.make_async_copy(b_ref.at[s], b_hbm.at[s], sems.at[2, k]) for k, s in enumerate(spans)]
    for copy in arrive:
        copy.start()
    chosen = choose(width, samp, 0, place_ref[0] != 0)
    for k, span in enumerate(spans):
        arrive[k].wait()
        both = matmul(values_ref[span, :], chosen).astype(jnp.bfloat16)
        a_ref[span, :] = both[:, :LANES]
        b_ref[span, :] = both[:, LANES:]
        leave[k].start()
        leave[blocks + k].start()
    for copy in leave:
        copy.wait()


def pick_kernel(samp, j, place_ref, values_ref, a_ref, b_ref):
    rows, width = values_ref.shape
    chosen = choose(width, samp, j, place_ref[0] != 0)
    for k in range(0, rows, DEPTH):
        span = pl.ds(k, DEPTH)
        both = matmul(values_ref[span, :], chosen).astype(jnp.bfloat16)
        a_ref[span, :] = both[:, :LANES]
        b_ref[span, :] = both[:, LANES:]


def final_kernel(samples, chunks, share, tile_ref, kept_ref, other_ref, early_ref, far0_ref, far1_ref, *rest):
    nears, out_ref = rest[:-1], rest[-1]
    part = tile_ref.shape[0]
    step = LANES
    scale = 1.0 / samples
    out_ref[0] = tile_ref[...] * scale
    for j, near_ref in enumerate(nears):
        out_ref[1, :, j * step : (j + 1) * step] = near_ref[:part, :] * scale
    out_ref[1, :, len(nears) * step :] = (kept_ref[0, :part, :] + other_ref[...]) * scale
    at = 0
    for j in range(chunks):
        names = [(i, j) for i in range(j)] + [(j, j)] + [(j, i) for i in range(j)]
        if j == chunks - 1:
            at = 0
        for row, column in names:
            rows = slice(at, at + share)
            piece = early_ref[rows, :] if j < chunks - 1 else far0_ref[rows, :] + far1_ref[rows, :]
            out_ref[2, row * share : (row + 1) * share, column * step : (column + 1) * step] = piece * scale
            at += share


def own_kernel(samp, place_ref, values_ref, mean_ref, scale_ref, own_ref, *outs):
    rows, width = values_ref.shape
    part = width // samp
    total = None
    for k in range(0, rows, DEPTH):
        span = pl.ds(k, DEPTH)
        z = ((values_ref[span, :].astype(jnp.float32) - mean_ref[...]) * scale_ref[...]).astype(jnp.bfloat16)
        flat = z.T
        own_ref[:, span] = flat
        total = accumulate(total, [matmul(flat, z)])
    parts = [total[0][t * part : (t + 1) * part] for t in range(samp)]
    for out_ref, value in zip(outs, by_distance(parts, place_ref[1])):
        out_ref[...] = value


def step_kernel(samp, j, results, place_ref, sa_ref, sb_ref, a_ref, b_ref, own_ref, *rest):
    nears, fars = rest[:j], rest[j : 2 * j]
    saved, outs = rest[2 * j : len(rest) - results], rest[len(rest) - results :]
    rows, step = a_ref.shape
    part, share = own_ref.shape[0] // samp, step // samp
    even, me = place_ref[0] != 0, place_ref[1]
    cols = pl.ds(j * step, step)
    sa, sb = sa_ref[:, cols], sb_ref[:, cols]
    after = jnp.where(even, sa, sb)
    before = jnp.where(even, sb, sa)
    total = None
    for k in range(0, rows, DEPTH):
        span = pl.ds(k, DEPTH)
        a, b = a_ref[span, :].astype(jnp.float32), b_ref[span, :].astype(jnp.float32)
        near = ((jnp.where(even, a, b) - after[0:1]) * after[1:2]).astype(jnp.bfloat16)
        far = ((jnp.where(even, b, a) - before[2:3]) * before[3:4]).astype(jnp.bfloat16).T
        if saved:
            saved[0][span, :] = near
            saved[1][:, span] = far
        terms = [matmul(own_ref[:, span], near)]
        terms += [matmul(fars[i][:, span], near) for i in range(j)]
        terms += [matmul(far, jnp.concatenate([near] + [nears[i][span, :] for i in range(j)], 1))]
        total = accumulate(total, terms)
    blocks = total[1:-1] + [total[-1][:, i * step : (i + 1) * step] for i in range(j + 1)]
    parts = [
        [total[0][t * part : (t + 1) * part]] + [block[t * share : (t + 1) * share] for block in blocks]
        for t in range(samp)
    ]
    parts = [by_distance([parts[t][n] for t in range(samp)], me) for n in range(len(blocks) + 1)]
    if len(outs) != samp:
        outs = [outs[d % 2].at[d // 2] for d in range(samp)]
    for d, out_ref in enumerate(outs):
        row = 0
        for piece in parts:
            size = piece[d].shape[0]
            out_ref[row : row + size, :] = piece[d]
            row += size


def call(kernel, out_shapes, flops, *args, scalars=True, in_hbm=(), scratch=(), out_space=pltpu.VMEM, limit=None):
    vmem = pl.BlockSpec(memory_space=pltpu.VMEM)
    specs = [vmem] * len(args)
    if scalars:
        specs[0] = pl.BlockSpec(memory_space=pltpu.SMEM)
    for n in in_hbm:
        specs[n] = pl.BlockSpec(memory_space=pltpu.HBM)
    moved = sum(x.size * x.dtype.itemsize for x in args) + sum(x.size * x.dtype.itemsize for x in out_shapes)
    return pl.pallas_call(
        kernel,
        out_shape=out_shapes,
        in_specs=specs,
        out_specs=[pl.BlockSpec(memory_space=out_space)] * len(out_shapes),
        scratch_shapes=scratch,
        cost_estimate=pl.CostEstimate(flops=flops, bytes_accessed=moved, transcendentals=0),
        compiler_params=pltpu.CompilerParams(vmem_limit_bytes=limit or VMEM_LIMIT),
    )(*args)


VMEM_LIMIT = 20 * 2**20
FRONT_LIMIT = 54 * 2**20


def body(dosage, filter_mask, counts):
    chain, samp = lax.axis_size("chain"), lax.axis_size("samp")
    me, block = lax.axis_index("samp"), lax.axis_index("chain")
    even = block % 2 == 0
    place = jnp.stack([even.astype(jnp.int32), me.astype(jnp.int32)])
    local_rows, width = dosage.shape
    samples = local_rows * samp
    step = LANES
    chunks = width // step
    part = width // samp
    share = step // samp

    def spread(vector):
        lead = vector.shape[:-1]
        grid = vector.reshape(*lead, samp, chunks, share)
        return jnp.swapaxes(grid, -3, -2).reshape(*lead, width)

    def scatter_sum(parts):
        total = parts[0]
        for d in range(1, samp):
            total = total + lax.ppermute(parts[d], "samp", [(i, i ^ d) for i in range(samp)])
        return total

    def f32(*shape):
        return jax.ShapeDtypeStruct(shape, jnp.float32)

    def bf16(*shape):
        return jax.ShapeDtypeStruct(shape, jnp.bfloat16)

    raw = []
    chunk = bf16(local_rows, step)
    flops = 4 * local_rows * width * step
    for j in range(chunks):
        if j == 0:
            a, b = call(
                functools.partial(front_kernel, samp), [chunk, chunk], flops, place, dosage, in_hbm=(1,),
                out_space=pltpu.HBM, limit=FRONT_LIMIT,
                scratch=[
                    pltpu.VMEM(dosage.shape, dosage.dtype),
                    pltpu.VMEM(chunk.shape, chunk.dtype),
                    pltpu.VMEM(chunk.shape, chunk.dtype),
                    pltpu.SemaphoreType.DMA((3, BLOCKS)),
                ],
            )
        else:
            a, b = call(functools.partial(pick_kernel, samp, j), [chunk, chunk], flops, place, dosage)
        a = exchange(a, chain, 0)
        b = exchange(b, chain, 1)
        raw.append((a, b))

    values = dosage.astype(jnp.float32)
    totals, squares = lax.psum((jnp.sum(values, 0), jnp.sum(values * values, 0)), "samp")
    mean = totals / samples
    var = squares / samples - mean * mean
    live = (jnp.arange(width, dtype=jnp.int32) < counts[0]).astype(jnp.float32)
    keep = filter_mask.astype(jnp.float32) * live
    scale = lax.rsqrt(var + 1e-05) * keep
    stats = jnp.stack([mean, scale])
    stats = jnp.concatenate([stats, spread(stats)])
    sa = exchange(stats, chain, 0)
    sb = exchange(stats, chain, 1)

    own, *parts = call(
        functools.partial(own_kernel, samp),
        [bf16(width, local_rows)] + [f32(part, width)] * samp,
        2 * local_rows * width * width,
        place, dosage, mean[None], scale[None],
    )
    tile = scatter_sum(parts)

    nears, fars, totals = [], [], []
    for j in range(chunks):
        size = part + (2 * j + 1) * share
        last = j == chunks - 1
        results = [f32(samp // 2, size, step)] * 2 if last else [f32(size, step)] * samp
        saved = [] if last else [bf16(local_rows, step), bf16(step, local_rows)]
        kept = call(
            functools.partial(step_kernel, samp, j, len(results)),
            saved + results,
            2 * local_rows * step * (width + (2 * j + 1) * step),
            place, sa, sb, *raw[j], own, *nears, *fars,
        )
        parts = kept[len(saved) :]
        if not last:
            nears.append(kept[0])
            fars.append(kept[1])
            totals.append(scatter_sum(parts))
    early = lax.ppermute(
        jnp.concatenate([total[part:] for total in totals]), "chain", [(i + 1, i) for i in range(chain - 1)]
    )
    kept = parts[0] + lax.ppermute(parts[1], "samp", [(i, i ^ 1) for i in range(samp)])
    others, far = [], []
    for n in range(samp // 2):
        moved = [i ^ (2 * n) for i in range(samp)]
        pairs = [((c + 1) * samp + i, c * samp + moved[i]) for c in range(chain - 1) for i in range(samp)]
        far.append(lax.ppermute(kept[n, part:], ("chain", "samp"), pairs))
        if n:
            others.append(lax.ppermute(kept[n, :part], "samp", [(i, moved[i]) for i in range(samp)]))
    (out,) = call(
        functools.partial(final_kernel, samples, chunks, share),
        [f32(3, part, width)],
        0,
        tile, kept, sum(others), early, far[0], sum(far[1:]), *totals,
        scalars=False,
    )
    return jnp.swapaxes(out, 0, 1)[None]


def solution(mesh):
    in_specs = (P("samp", ("groups", "chain")), P(("groups", "chain")), P(("groups", "chain")))
    out_specs = P(("groups", "chain"), "samp", None, None)
    return jax.shard_map(body, mesh=mesh, in_specs=in_specs, out_specs=out_specs, check_vma=False)
```

```python
import functools

import jax
import jax.numpy as jnp
from jax import lax
from jax.experimental import pallas as pl
from jax.experimental.pallas import tpu as pltpu
from jax.sharding import PartitionSpec as P


LANES = 128
DEPTH = 1024


def exchange(array, devices, first):
    pairs = []
    for low in range(first, devices - 1, 2):
        pairs += [(low, low + 1), (low + 1, low)]
    return lax.ppermute(array, "chain", pairs) if pairs else jnp.zeros_like(array)


def matmul(left, right):
    return lax.dot_general(left, right, (((1,), (0,)), ((), ())), preferred_element_type=jnp.float32)


def accumulate(total, terms):
    return terms if total is None else [t + u for t, u in zip(total, terms)]


def by_distance(parts, me):
    bit = 1
    while bit < len(parts):
        swap = (me // bit) % 2 == 1
        parts = [jnp.where(swap, parts[t ^ bit], parts[t]) for t in range(len(parts))]
        bit *= 2
    return parts


def choose(width, samp, j, even):
    step = LANES
    part, share = width // samp, step // samp
    lane = lax.broadcasted_iota(jnp.int32, (width, step), 1)
    row = lax.broadcasted_iota(jnp.int32, (width, step), 0)
    up = lane // share * part + j * share + lane % share
    down = j * step + lane
    first, second = jnp.where(even, up, down), jnp.where(even, down, up)
    return jnp.concatenate([row == first, row == second], 1).astype(jnp.float32).astype(jnp.bfloat16)


def pick_kernel(samp, j, place_ref, values_ref, a_ref, b_ref):
    rows, width = values_ref.shape
    skip = rows - a_ref.shape[0]
    chosen = choose(width, samp, j, place_ref[0] != 0)
    for k in range(0, rows - skip, DEPTH):
        span = pl.ds(k, DEPTH)
        both = matmul(values_ref[pl.ds(skip + k, DEPTH), :], chosen).astype(jnp.bfloat16)
        a_ref[span, :] = both[:, :LANES]
        b_ref[span, :] = both[:, LANES:]


def final_kernel(samples, chunks, share, tile_ref, kept_ref, other_ref, early_ref, far0_ref, far1_ref, *rest):
    nears, out_ref = rest[:-1], rest[-1]
    part = tile_ref.shape[0]
    step = LANES
    scale = 1.0 / samples
    out_ref[0] = tile_ref[...] * scale
    for j, near_ref in enumerate(nears):
        out_ref[1, :, j * step : (j + 1) * step] = near_ref[:part, :] * scale
    out_ref[1, :, len(nears) * step :] = (kept_ref[0, :part, :] + other_ref[...]) * scale
    at = 0
    for j in range(chunks):
        names = [(i, j) for i in range(j)] + [(j, j)] + [(j, i) for i in range(j)]
        if j == chunks - 1:
            at = 0
        for row, column in names:
            rows = slice(at, at + share)
            piece = early_ref[rows, :] if j < chunks - 1 else far0_ref[rows, :] + far1_ref[rows, :]
            out_ref[2, row * share : (row + 1) * share, column * step : (column + 1) * step] = piece * scale
            at += share


def own_kernel(samp, place_ref, values_ref, mean_ref, scale_ref, own_ref, *outs):
    rows, width = values_ref.shape
    part = width // samp
    total = None
    for k in range(0, rows, DEPTH):
        span = pl.ds(k, DEPTH)
        z = ((values_ref[span, :].astype(jnp.float32) - mean_ref[...]) * scale_ref[...]).astype(jnp.bfloat16)
        flat = z.T
        own_ref[:, span] = flat
        total = accumulate(total, [matmul(flat, z)])
    parts = [total[0][t * part : (t + 1) * part] for t in range(samp)]
    for out_ref, value in zip(outs, by_distance(parts, place_ref[1])):
        out_ref[...] = value


def base_kernel(place_ref, sa_ref, sb_ref, own_ref, *rest):
    raw, (near_out, far_out) = rest[:-2], rest[-2:]
    even = place_ref[0] != 0
    after = jnp.where(even, sa_ref[...], sb_ref[...])
    before = jnp.where(even, sb_ref[...], sa_ref[...])
    total, at = None, 0
    for a_ref, b_ref in zip(raw[::2], raw[1::2]):
        rows = a_ref.shape[0]
        for k in range(0, rows, min(rows, DEPTH // 2)):
            size = min(rows, DEPTH // 2)
            span = pl.ds(k, size)
            a, b = a_ref[span, :].astype(jnp.float32), b_ref[span, :].astype(jnp.float32)
            near = ((jnp.where(even, a, b) - after[0:1]) * after[1:2]).astype(jnp.bfloat16)
            far = ((jnp.where(even, b, a) - before[0:1]) * before[1:2]).astype(jnp.bfloat16).T
            total = accumulate(total, [matmul(own_ref[:, pl.ds(at, size)], near), matmul(far, near)])
            at += size
    near_out[...] = total[0]
    far_out[...] = total[1]


def step_kernel(samp, j, results, place_ref, sa_ref, sb_ref, a_ref, b_ref, own_ref, base_near, base_far, *rest):
    nears, fars = rest[:j], rest[j : 2 * j]
    saved, outs = rest[2 * j : len(rest) - results], rest[len(rest) - results :]
    rows, step = a_ref.shape
    skip = own_ref.shape[1] - rows
    part, share = own_ref.shape[0] // samp, step // samp
    even, me = place_ref[0] != 0, place_ref[1]
    cols = pl.ds(j * step, step)
    sa, sb = sa_ref[:, cols], sb_ref[:, cols]
    after = jnp.where(even, sa, sb)
    before = jnp.where(even, sb, sa)
    total = None
    for k in range(0, rows, DEPTH):
        span = pl.ds(k, DEPTH)
        a, b = a_ref[span, :].astype(jnp.float32), b_ref[span, :].astype(jnp.float32)
        near = ((jnp.where(even, a, b) - after[0:1]) * after[1:2]).astype(jnp.bfloat16)
        far = ((jnp.where(even, b, a) - before[2:3]) * before[3:4]).astype(jnp.bfloat16).T
        if saved:
            saved[0][span, :] = near
            saved[1][:, span] = far
        terms = [matmul(own_ref[:, pl.ds(skip + k, DEPTH)], near)]
        terms += [matmul(fars[i][:, span], near) for i in range(j)]
        terms += [matmul(far, jnp.concatenate([near] + [nears[i][span, :] for i in range(j)], 1))]
        total = accumulate(total, terms)
    blocks = total[1:-1] + [total[-1][:, i * step : (i + 1) * step] for i in range(j + 1)]
    names = [(i, j) for i in range(j)] + [(j, j)] + [(j, i) for i in range(j)]
    parts = []
    for t in range(samp):
        parts.append([total[0][t * part : (t + 1) * part] + base_near[t * part : (t + 1) * part, cols]])
        for block, (row, column) in zip(blocks, names):
            first = t * part + row * share
            base = base_far[first : first + share, column * step : (column + 1) * step]
            parts[t].append(block[t * share : (t + 1) * share] + base)
    parts = [by_distance([parts[t][n] for t in range(samp)], me) for n in range(len(blocks) + 1)]
    if len(outs) != samp:
        outs = [outs[d % 2].at[d // 2] for d in range(samp)]
    for d, out_ref in enumerate(outs):
        row = 0
        for piece in parts:
            size = piece[d].shape[0]
            out_ref[row : row + size, :] = piece[d]
            row += size


def call(kernel, out_shapes, flops, *args, scalars=True):
    vmem = pl.BlockSpec(memory_space=pltpu.VMEM)
    specs = [vmem] * len(args)
    if scalars:
        specs[0] = pl.BlockSpec(memory_space=pltpu.SMEM)
    moved = sum(x.size * x.dtype.itemsize for x in args) + sum(x.size * x.dtype.itemsize for x in out_shapes)
    return pl.pallas_call(
        kernel,
        out_shape=out_shapes,
        in_specs=specs,
        out_specs=[vmem] * len(out_shapes),
        cost_estimate=pl.CostEstimate(flops=flops, bytes_accessed=moved, transcendentals=0),
        compiler_params=pltpu.CompilerParams(vmem_limit_bytes=VMEM_LIMIT),
    )(*args)


VMEM_LIMIT = 20 * 2**20


def body(dosage, filter_mask, counts):
    chain, samp = lax.axis_size("chain"), lax.axis_size("samp")
    me, block = lax.axis_index("samp"), lax.axis_index("chain")
    even = block % 2 == 0
    place = jnp.stack([even.astype(jnp.int32), me.astype(jnp.int32)])
    local_rows, width = dosage.shape
    samples = local_rows * samp
    step = LANES
    chunks = width // step
    part = width // samp
    share = step // samp

    def spread(vector):
        lead = vector.shape[:-1]
        grid = vector.reshape(*lead, samp, chunks, share)
        return jnp.swapaxes(grid, -3, -2).reshape(*lead, width)

    def scatter_sum(parts):
        total = parts[0]
        for d in range(1, samp):
            total = total + lax.ppermute(parts[d], "samp", [(i, i ^ d) for i in range(samp)])
        return total

    def f32(*shape):
        return jax.ShapeDtypeStruct(shape, jnp.float32)

    def bf16(*shape):
        return jax.ShapeDtypeStruct(shape, jnp.bfloat16)

    half = local_rows // 2
    first = half // 4
    heads = []
    for low, high in [(0, first), (first, half)]:
        piece = dosage[low:high]
        piece, dosage = lax.optimization_barrier((piece, dosage))
        heads.append(exchange(piece, chain, 0))
        heads.append(exchange(piece, chain, 1))
    raw = []
    chunk = bf16(half, step)
    for j in range(chunks):
        a, b = call(functools.partial(pick_kernel, samp, j), [chunk, chunk], 4 * half * width * step, place, dosage)
        a = exchange(a, chain, 0)
        b = exchange(b, chain, 1)
        raw.append((a, b))

    values = dosage.astype(jnp.float32)
    totals, squares = lax.psum((jnp.sum(values, 0), jnp.sum(values * values, 0)), "samp")
    mean = totals / samples
    var = squares / samples - mean * mean
    live = (jnp.arange(width, dtype=jnp.int32) < counts[0]).astype(jnp.float32)
    keep = filter_mask.astype(jnp.float32) * live
    scale = lax.rsqrt(var + 1e-05) * keep
    stats = jnp.stack([mean, scale])
    stats = jnp.concatenate([stats, spread(stats)])
    sa = exchange(stats, chain, 0)
    sb = exchange(stats, chain, 1)

    own, *parts = call(
        functools.partial(own_kernel, samp),
        [bf16(width, local_rows)] + [f32(part, width)] * samp,
        2 * local_rows * width * width,
        place, dosage, mean[None], scale[None],
    )
    tile = scatter_sum(parts)

    base = call(base_kernel, [f32(width, width)] * 2, 4 * half * width * width, place, sa, sb, own, *heads)
    nears, fars, totals = [], [], []
    for j in range(chunks):
        size = part + (2 * j + 1) * share
        last = j == chunks - 1
        results = [f32(samp // 2, size, step)] * 2 if last else [f32(size, step)] * samp
        saved = [] if last else [bf16(half, step), bf16(step, half)]
        kept = call(
            functools.partial(step_kernel, samp, j, len(results)),
            saved + results,
            2 * half * step * (width + (2 * j + 1) * step),
            place, sa, sb, *raw[j], own, *base, *nears, *fars,
        )
        parts = kept[len(saved) :]
        if not last:
            nears.append(kept[0])
            fars.append(kept[1])
            totals.append(scatter_sum(parts))
    early = lax.ppermute(
        jnp.concatenate([total[part:] for total in totals]), "chain", [(i + 1, i) for i in range(chain - 1)]
    )
    kept = parts[0] + lax.ppermute(parts[1], "samp", [(i, i ^ 1) for i in range(samp)])
    others, far = [], []
    for n in range(samp // 2):
        moved = [i ^ (2 * n) for i in range(samp)]
        pairs = [((c + 1) * samp + i, c * samp + moved[i]) for c in range(chain - 1) for i in range(samp)]
        far.append(lax.ppermute(kept[n, part:], ("chain", "samp"), pairs))
        if n:
            others.append(lax.ppermute(kept[n, :part], "samp", [(i, moved[i]) for i in range(samp)]))
    (out,) = call(
        functools.partial(final_kernel, samples, chunks, share),
        [f32(3, part, width)],
        0,
        tile, kept, sum(others), early, far[0], sum(far[1:]), *totals,
        scalars=False,
    )
    return jnp.swapaxes(out, 0, 1)[None]


def solution(mesh):
    in_specs = (P("samp", ("groups", "chain")), P(("groups", "chain")), P(("groups", "chain")))
    out_specs = P(("groups", "chain"), "samp", None, None)
    return jax.shard_map(body, mesh=mesh, in_specs=in_specs, out_specs=out_specs, check_vma=False)
```

```python
import functools

import jax
import jax.numpy as jnp
from jax import lax
from jax.experimental import pallas as pl
from jax.experimental.pallas import tpu as pltpu
from jax.sharding import PartitionSpec as P


LANES = 128
DEPTH = 1024


def exchange(array, devices, first):
    pairs = []
    for low in range(first, devices - 1, 2):
        pairs += [(low + 1, low)] if low + 2 == devices else [(low, low + 1), (low + 1, low)]
    return lax.ppermute(array, "chain", pairs) if pairs else jnp.zeros_like(array)


def matmul(left, right):
    return lax.dot_general(left, right, (((1,), (0,)), ((), ())), preferred_element_type=jnp.float32)


def accumulate(total, terms):
    return terms if total is None else [t + u for t, u in zip(total, terms)]


def by_distance(parts, me):
    bit = 1
    while bit < len(parts):
        swap = (me // bit) % 2 == 1
        parts = [jnp.where(swap, parts[t ^ bit], parts[t]) for t in range(len(parts))]
        bit *= 2
    return parts


def choose(width, samp, j, even):
    step = LANES
    part, share = width // samp, step // samp
    lane = lax.broadcasted_iota(jnp.int32, (width, step), 1)
    row = lax.broadcasted_iota(jnp.int32, (width, step), 0)
    up = lane // share * part + j * share + lane % share
    down = j * step + lane
    first, second = jnp.where(even, up, down), jnp.where(even, down, up)
    return jnp.concatenate([row == first, row == second], 1).astype(jnp.float32).astype(jnp.bfloat16)


def pick_kernel(samp, j, place_ref, values_ref, a_ref, b_ref):
    rows, width = values_ref.shape
    skip = rows - a_ref.shape[0]
    chosen = choose(width, samp, j, place_ref[0] != 0)
    for k in range(0, rows - skip, DEPTH):
        span = pl.ds(k, DEPTH)
        both = matmul(values_ref[pl.ds(skip + k, DEPTH), :], chosen).astype(jnp.bfloat16)
        a_ref[span, :] = both[:, :LANES]
        b_ref[span, :] = both[:, LANES:]


def final_kernel(samples, chunks, share, tile_ref, near_ref, other_ref, early_ref, far_ref, rest_ref, *rest):
    nears, out_ref = rest[:-1], rest[-1]
    part = tile_ref.shape[0]
    step = LANES
    scale = 1.0 / samples
    out_ref[0] = tile_ref[...] * scale
    for j, done_ref in enumerate(nears):
        out_ref[1, :, j * step : (j + 1) * step] = done_ref[:part, :] * scale
    out_ref[1, :, len(nears) * step :] = (near_ref[0] + other_ref[...]) * scale
    at = 0
    for j in range(chunks):
        if j == chunks - 1:
            at = 0
        for row, column in far_names(j):
            rows = slice(at, at + share)
            piece = early_ref[rows, :] if j < chunks - 1 else far_ref[0, rows, :] + rest_ref[rows, :]
            out_ref[2, row * share : (row + 1) * share, column * step : (column + 1) * step] = piece * scale
            at += share


def by_route(parts, me):
    if len(parts) != 4:
        return by_distance(parts, me)
    chip, core = me // 2 == 1, me % 2 == 1
    near = [jnp.where(core, parts[2 + n], parts[n]) for n in range(2)]
    away = [jnp.where(core, parts[n], parts[2 + n]) for n in range(2)]
    near = [jnp.where(chip, near[1 - n], near[n]) for n in range(2)]
    away = [jnp.where(chip, away[1 - n], away[n]) for n in range(2)]
    return [near[0], away[0], near[1], away[1]]


def own_kernel(samp, place_ref, values_ref, mean_ref, scale_ref, own_ref, *outs):
    rows, width = values_ref.shape
    part = width // samp
    total = None
    for k in range(0, rows, DEPTH):
        span = pl.ds(k, DEPTH)
        z = ((values_ref[span, :].astype(jnp.float32) - mean_ref[...]) * scale_ref[...]).astype(jnp.bfloat16)
        flat = z.T
        own_ref[:, span] = flat
        total = accumulate(total, [matmul(flat, z)])
    store(outs, by_distance([total[0][t * part : (t + 1) * part] for t in range(samp)], place_ref[1]), 0)


def store(outs, values, row):
    for d, value in enumerate(values):
        outs[d % 2][d // 2, row : row + value.shape[0], :] = value
    return row + values[0].shape[0]


def base_kernel(place_ref, sa_ref, sb_ref, own_ref, *rest):
    raw, (near_out, far_out) = rest[:-2], rest[-2:]
    even = place_ref[0] != 0
    after = jnp.where(even, sa_ref[...], sb_ref[...])
    before = jnp.where(even, sb_ref[...], sa_ref[...])
    total, at = None, 0
    for a_ref, b_ref in zip(raw[::2], raw[1::2]):
        rows = a_ref.shape[0]
        for k in range(0, rows, min(rows, DEPTH // 2)):
            size = min(rows, DEPTH // 2)
            span = pl.ds(k, size)
            a, b = a_ref[span, :].astype(jnp.float32), b_ref[span, :].astype(jnp.float32)
            near = ((jnp.where(even, a, b) - after[0:1]) * after[1:2]).astype(jnp.bfloat16)
            far = ((jnp.where(even, b, a) - before[0:1]) * before[1:2]).astype(jnp.bfloat16).T
            total = accumulate(total, [matmul(own_ref[:, pl.ds(at, size)], near), matmul(far, near)])
            at += size
    near_out[...] = total[0]
    far_out[...] = total[1]


def step_kernel(samp, j, whole, place_ref, sa_ref, sb_ref, a_ref, b_ref, own_ref, base_near, base_far, *rest):
    nears, fars, near_ref, saved, outs = rest[:j], rest[j : 2 * j], rest[2 * j], rest[2 * j + 1 : -2], rest[-2:]
    rows, step = a_ref.shape
    skip = own_ref.shape[1] - rows
    part, share = own_ref.shape[0] // samp, step // samp
    even, me = place_ref[0] != 0, place_ref[1]
    cols = pl.ds(j * step, step)
    sa, sb = sa_ref[:, cols], sb_ref[:, cols]
    after = jnp.where(even, sa, sb)
    before = jnp.where(even, sb, sa)
    total = None
    for k in range(0, rows, DEPTH):
        span = pl.ds(k, DEPTH)
        a, b = a_ref[span, :].astype(jnp.float32), b_ref[span, :].astype(jnp.float32)
        near = ((jnp.where(even, a, b) - after[0:1]) * after[1:2]).astype(jnp.bfloat16)
        far = ((jnp.where(even, b, a) - before[2:3]) * before[3:4]).astype(jnp.bfloat16).T
        near_ref[span, :] = near
        if whole:
            saved[0][:, span] = far
        terms = [matmul(own_ref[:, pl.ds(skip + k, DEPTH)], near)] if whole else []
        terms += [matmul(fars[i][:, span], near) for i in range(j)]
        terms += [matmul(far, jnp.concatenate([near] + [nears[i][span, :] for i in range(j)], 1))]
        total = accumulate(total, terms)
    row = 0
    if whole:
        row = store(outs, near_parts(samp, total.pop(0), base_near, me, cols), row)
    blocks = total[:-1] + [total[-1][:, i * step : (i + 1) * step] for i in range(j + 1)]
    for block, (up, down) in zip(blocks, far_names(j)):
        parts = []
        for t in range(samp):
            first = t * part + up * share
            base = base_far[first : first + share, down * step : (down + 1) * step]
            parts.append(block[t * share : (t + 1) * share] + base)
        row = store(outs, by_distance(parts, me) if whole else by_route(parts, me), row)


def near_parts(samp, tile, base_near, me, cols):
    part = tile.shape[0] // samp
    spans = [slice(t * part, (t + 1) * part) for t in range(samp)]
    return by_distance([tile[span] + base_near[span, cols] for span in spans], me)


def near_kernel(samp, j, place_ref, near_ref, own_ref, base_near, *outs):
    rows, step = near_ref.shape
    skip = own_ref.shape[1] - rows
    tile = matmul(own_ref[:, pl.ds(skip, rows)], near_ref[...])
    store(outs, near_parts(samp, tile, base_near, place_ref[1], pl.ds(j * step, step)), 0)


def far_names(j):
    return [(i, j) for i in range(j)] + [(j, j)] + [(j, i) for i in range(j)]


def call(kernel, out_shapes, flops, *args, scalars=True):
    vmem = pl.BlockSpec(memory_space=pltpu.VMEM)
    specs = [vmem] * len(args)
    if scalars:
        specs[0] = pl.BlockSpec(memory_space=pltpu.SMEM)
    moved = sum(x.size * x.dtype.itemsize for x in args) + sum(x.size * x.dtype.itemsize for x in out_shapes)
    return pl.pallas_call(
        kernel,
        out_shape=out_shapes,
        in_specs=specs,
        out_specs=[vmem] * len(out_shapes),
        cost_estimate=pl.CostEstimate(flops=flops, bytes_accessed=moved, transcendentals=0),
        compiler_params=pltpu.CompilerParams(vmem_limit_bytes=VMEM_LIMIT),
    )(*args)


VMEM_LIMIT = 20 * 2**20


def body(dosage, filter_mask, counts):
    chain, samp = lax.axis_size("chain"), lax.axis_size("samp")
    me, block = lax.axis_index("samp"), lax.axis_index("chain")
    even = block % 2 == 0
    place = jnp.stack([even.astype(jnp.int32), me.astype(jnp.int32)])
    local_rows, width = dosage.shape
    samples = local_rows * samp
    step = LANES
    chunks = width // step
    part = width // samp
    share = step // samp

    def spread(vector):
        lead = vector.shape[:-1]
        grid = vector.reshape(*lead, samp, chunks, share)
        return jnp.swapaxes(grid, -3, -2).reshape(*lead, width)

    def swap(array, distance):
        return lax.ppermute(array, "samp", [(i, i ^ distance) for i in range(samp)])

    def scatter_sum(kept, sent):
        kept = kept + swap(sent, 1)
        total = kept[0]
        for n in range(1, samp // 2):
            total = total + swap(kept[n], 2 * n)
        return total

    def f32(*shape):
        return jax.ShapeDtypeStruct(shape, jnp.float32)

    def bf16(*shape):
        return jax.ShapeDtypeStruct(shape, jnp.bfloat16)

    half = local_rows // 2
    first = half // 4
    heads = []
    for low, high in [(0, first), (first, half)]:
        piece = dosage[low:high]
        piece, dosage = lax.optimization_barrier((piece, dosage))
        heads.append(exchange(piece, chain, 0))
        heads.append(exchange(piece, chain, 1))
    raw = []
    chunk = bf16(half, step)
    for j in range(chunks):
        a, b = call(functools.partial(pick_kernel, samp, j), [chunk, chunk], 4 * half * width * step, place, dosage)
        a = exchange(a, chain, 0)
        b = exchange(b, chain, 1)
        raw.append((a, b))

    values = dosage.astype(jnp.float32)
    totals, squares = lax.psum((jnp.sum(values, 0), jnp.sum(values * values, 0)), "samp")
    mean = totals / samples
    var = squares / samples - mean * mean
    live = (jnp.arange(width, dtype=jnp.int32) < counts[0]).astype(jnp.float32)
    keep = filter_mask.astype(jnp.float32) * live
    scale = lax.rsqrt(var + 1e-05) * keep
    stats = jnp.stack([mean, scale])
    stats = jnp.concatenate([stats, spread(stats)])
    sa = exchange(stats, chain, 0)
    sb = exchange(stats, chain, 1)

    own, *parts = call(
        functools.partial(own_kernel, samp),
        [bf16(width, local_rows)] + [f32(samp // 2, part, width)] * 2,
        2 * local_rows * width * width,
        place, dosage, mean[None], scale[None],
    )
    tile = scatter_sum(*parts)

    base = call(base_kernel, [f32(width, width)] * 2, 4 * half * width * width, place, sa, sb, own, *heads)
    nears, fars, totals = [], [], []
    for j in range(chunks):
        blocks = (2 * j + 1) * share
        last = j == chunks - 1
        near, *saved, kept, sent = call(
            functools.partial(step_kernel, samp, j, not last),
            [bf16(half, step)]
            + ([] if last else [bf16(step, half)])
            + [f32(samp // 2, blocks + (0 if last else part), step)] * 2,
            2 * half * step * ((0 if last else width) + (2 * j + 1) * step),
            place, sa, sb, *raw[j], own, *base, *nears, *fars,
        )
        if not last:
            nears.append(near)
            fars += saved
            totals.append(scatter_sum(kept, sent))
    early = lax.ppermute(
        jnp.concatenate([total[part:] for total in totals]), "chain", [(i + 1, i) for i in range(chain - 2)]
    )
    kept = kept + swap(sent, 1)
    near, sent = call(
        functools.partial(near_kernel, samp, chunks - 1), [f32(samp // 2, part, step)] * 2, 2 * half * step * width,
        place, near, own, base[0],
    )
    near = near + swap(sent, 1)

    def down(array, moved):
        pairs = [((c + 1) * samp + i, c * samp + moved(i)) for c in range(chain - 2) for i in range(samp)]
        return lax.ppermute(array, ("chain", "samp"), pairs)

    if samp == 4:
        far = down(kept, lambda i: i % 2 * 2 + i // 2)
        rest = swap(far[1], 1)
    else:
        rest = sum(down(kept[n], lambda i: i ^ (2 * n)) for n in range(1, samp // 2))
        far = down(kept[:1], lambda i: i)
    other = sum(swap(near[n], 2 * n) for n in range(1, samp // 2))
    (out,) = call(
        functools.partial(final_kernel, samples, chunks, share),
        [f32(3, part, width)],
        0,
        tile, near, other, early, far, rest, *totals,
        scalars=False,
    )
    return jnp.swapaxes(out, 0, 1)[None]


def solution(mesh):
    in_specs = (P("samp", ("groups", "chain")), P(("groups", "chain")), P(("groups", "chain")))
    out_specs = P(("groups", "chain"), "samp", None, None)
    return jax.shard_map(body, mesh=mesh, in_specs=in_specs, out_specs=out_specs, check_vma=False)
```

```python
import functools

import jax
import jax.numpy as jnp
from jax import lax
from jax.experimental import pallas as pl
from jax.experimental.pallas import tpu as pltpu
from jax.sharding import PartitionSpec as P


LANES = 128
DEPTH = 1024


def exchange(array, devices, first):
    pairs = []
    for low in range(first, devices - 1, 2):
        pairs += [(low, low + 1), (low + 1, low)]
    return lax.ppermute(array, "chain", pairs) if pairs else jnp.zeros_like(array)


def matmul(left, right):
    return lax.dot_general(left, right, (((1,), (0,)), ((), ())), preferred_element_type=jnp.float32)


def accumulate(total, terms):
    return terms if total is None else [t + u for t, u in zip(total, terms)]


def by_distance(parts, me):
    bit = 1
    while bit < len(parts):
        swap = (me // bit) % 2 == 1
        parts = [jnp.where(swap, parts[t ^ bit], parts[t]) for t in range(len(parts))]
        bit *= 2
    return parts


def choose(width, samp, j, even):
    step = LANES
    part, share = width // samp, step // samp
    lane = lax.broadcasted_iota(jnp.int32, (width, step), 1)
    row = lax.broadcasted_iota(jnp.int32, (width, step), 0)
    up = lane // share * part + j * share + lane % share
    down = j * step + lane
    first, second = jnp.where(even, up, down), jnp.where(even, down, up)
    return jnp.concatenate([row == first, row == second], 1).astype(jnp.float32).astype(jnp.bfloat16)


def pick_kernel(samp, j, place_ref, values_ref, a_ref, b_ref):
    rows, width = values_ref.shape
    skip = rows - a_ref.shape[0]
    chosen = choose(width, samp, j, place_ref[0] != 0)
    for k in range(0, rows - skip, DEPTH):
        span = pl.ds(k, DEPTH)
        both = matmul(values_ref[pl.ds(skip + k, DEPTH), :], chosen).astype(jnp.bfloat16)
        a_ref[span, :] = both[:, :LANES]
        b_ref[span, :] = both[:, LANES:]


def final_kernel(samples, chunks, share, tile_ref, near_ref, other_ref, early_ref, far0_ref, far1_ref, *rest):
    nears, out_ref = rest[:-1], rest[-1]
    part = tile_ref.shape[0]
    step = LANES
    scale = 1.0 / samples
    out_ref[0] = tile_ref[...] * scale
    for j, done_ref in enumerate(nears):
        out_ref[1, :, j * step : (j + 1) * step] = done_ref[:part, :] * scale
    out_ref[1, :, len(nears) * step :] = (near_ref[0] + other_ref[...]) * scale
    at = 0
    for j in range(chunks):
        if j == chunks - 1:
            at = 0
        for row, column in far_names(j):
            rows = slice(at, at + share)
            piece = early_ref[rows, :] if j < chunks - 1 else far0_ref[rows, :] + far1_ref[rows, :]
            out_ref[2, row * share : (row + 1) * share, column * step : (column + 1) * step] = piece * scale
            at += share


def own_kernel(samp, place_ref, values_ref, mean_ref, scale_ref, own_ref, *outs):
    rows, width = values_ref.shape
    part = width // samp
    total = None
    for k in range(0, rows, DEPTH):
        span = pl.ds(k, DEPTH)
        z = ((values_ref[span, :].astype(jnp.float32) - mean_ref[...]) * scale_ref[...]).astype(jnp.bfloat16)
        flat = z.T
        own_ref[:, span] = flat
        total = accumulate(total, [matmul(flat, z)])
    store(outs, by_distance([total[0][t * part : (t + 1) * part] for t in range(samp)], place_ref[1]), 0)


def store(outs, values, row):
    for d, value in enumerate(values):
        outs[d % 2][d // 2, row : row + value.shape[0], :] = value
    return row + values[0].shape[0]


def base_kernel(place_ref, sa_ref, sb_ref, own_ref, *rest):
    raw, (near_out, far_out) = rest[:-2], rest[-2:]
    even = place_ref[0] != 0
    after = jnp.where(even, sa_ref[...], sb_ref[...])
    before = jnp.where(even, sb_ref[...], sa_ref[...])
    total, at = None, 0
    for a_ref, b_ref in zip(raw[::2], raw[1::2]):
        rows = a_ref.shape[0]
        for k in range(0, rows, min(rows, DEPTH // 2)):
            size = min(rows, DEPTH // 2)
            span = pl.ds(k, size)
            a, b = a_ref[span, :].astype(jnp.float32), b_ref[span, :].astype(jnp.float32)
            near = ((jnp.where(even, a, b) - after[0:1]) * after[1:2]).astype(jnp.bfloat16)
            far = ((jnp.where(even, b, a) - before[0:1]) * before[1:2]).astype(jnp.bfloat16).T
            total = accumulate(total, [matmul(own_ref[:, pl.ds(at, size)], near), matmul(far, near)])
            at += size
    near_out[...] = total[0]
    far_out[...] = total[1]


def step_kernel(samp, j, whole, place_ref, sa_ref, sb_ref, a_ref, b_ref, own_ref, base_near, base_far, *rest):
    nears, fars, near_ref, saved, outs = rest[:j], rest[j : 2 * j], rest[2 * j], rest[2 * j + 1 : -2], rest[-2:]
    rows, step = a_ref.shape
    skip = own_ref.shape[1] - rows
    part, share = own_ref.shape[0] // samp, step // samp
    even, me = place_ref[0] != 0, place_ref[1]
    cols = pl.ds(j * step, step)
    sa, sb = sa_ref[:, cols], sb_ref[:, cols]
    after = jnp.where(even, sa, sb)
    before = jnp.where(even, sb, sa)
    total = None
    for k in range(0, rows, DEPTH):
        span = pl.ds(k, DEPTH)
        a, b = a_ref[span, :].astype(jnp.float32), b_ref[span, :].astype(jnp.float32)
        near = ((jnp.where(even, a, b) - after[0:1]) * after[1:2]).astype(jnp.bfloat16)
        far = ((jnp.where(even, b, a) - before[2:3]) * before[3:4]).astype(jnp.bfloat16).T
        near_ref[span, :] = near
        if whole:
            saved[0][:, span] = far
        terms = [matmul(own_ref[:, pl.ds(skip + k, DEPTH)], near)] if whole else []
        terms += [matmul(fars[i][:, span], near) for i in range(j)]
        terms += [matmul(far, jnp.concatenate([near] + [nears[i][span, :] for i in range(j)], 1))]
        total = accumulate(total, terms)
    row = 0
    if whole:
        row = store(outs, near_parts(samp, total.pop(0), base_near, me, cols), row)
    blocks = total[:-1] + [total[-1][:, i * step : (i + 1) * step] for i in range(j + 1)]
    for block, (up, down) in zip(blocks, far_names(j)):
        parts = []
        for t in range(samp):
            first = t * part + up * share
            base = base_far[first : first + share, down * step : (down + 1) * step]
            parts.append(block[t * share : (t + 1) * share] + base)
        row = store(outs, by_distance(parts, me), row)


def near_parts(samp, tile, base_near, me, cols):
    part = tile.shape[0] // samp
    spans = [slice(t * part, (t + 1) * part) for t in range(samp)]
    return by_distance([tile[span] + base_near[span, cols] for span in spans], me)


def near_kernel(samp, j, place_ref, near_ref, own_ref, base_near, *outs):
    rows, step = near_ref.shape
    skip = own_ref.shape[1] - rows
    tile = matmul(own_ref[:, pl.ds(skip, rows)], near_ref[...])
    store(outs, near_parts(samp, tile, base_near, place_ref[1], pl.ds(j * step, step)), 0)


def far_names(j):
    return [(i, j) for i in range(j)] + [(j, j)] + [(j, i) for i in range(j)]


def call(kernel, out_shapes, flops, *args, scalars=True):
    vmem = pl.BlockSpec(memory_space=pltpu.VMEM)
    specs = [vmem] * len(args)
    if scalars:
        specs[0] = pl.BlockSpec(memory_space=pltpu.SMEM)
    moved = sum(x.size * x.dtype.itemsize for x in args) + sum(x.size * x.dtype.itemsize for x in out_shapes)
    return pl.pallas_call(
        kernel,
        out_shape=out_shapes,
        in_specs=specs,
        out_specs=[vmem] * len(out_shapes),
        cost_estimate=pl.CostEstimate(flops=flops, bytes_accessed=moved, transcendentals=0),
        compiler_params=pltpu.CompilerParams(vmem_limit_bytes=VMEM_LIMIT),
    )(*args)


VMEM_LIMIT = 20 * 2**20


def body(dosage, filter_mask, counts):
    chain, samp = lax.axis_size("chain"), lax.axis_size("samp")
    me, block = lax.axis_index("samp"), lax.axis_index("chain")
    even = block % 2 == 0
    place = jnp.stack([even.astype(jnp.int32), me.astype(jnp.int32)])
    local_rows, width = dosage.shape
    samples = local_rows * samp
    step = LANES
    chunks = width // step
    part = width // samp
    share = step // samp

    def spread(vector):
        lead = vector.shape[:-1]
        grid = vector.reshape(*lead, samp, chunks, share)
        return jnp.swapaxes(grid, -3, -2).reshape(*lead, width)

    def swap(array, distance):
        return lax.ppermute(array, "samp", [(i, i ^ distance) for i in range(samp)])

    def scatter_sum(kept, sent):
        kept = kept + swap(sent, 1)
        total = kept[0]
        for n in range(1, samp // 2):
            total = total + swap(kept[n], 2 * n)
        return total

    def f32(*shape):
        return jax.ShapeDtypeStruct(shape, jnp.float32)

    def bf16(*shape):
        return jax.ShapeDtypeStruct(shape, jnp.bfloat16)

    half = local_rows // 2
    first = half // 4
    heads = []
    for low, high in [(0, first), (first, half)]:
        piece = dosage[low:high]
        piece, dosage = lax.optimization_barrier((piece, dosage))
        heads.append(exchange(piece, chain, 0))
        heads.append(exchange(piece, chain, 1))
    raw = []
    chunk = bf16(half, step)
    for j in range(chunks):
        a, b = call(functools.partial(pick_kernel, samp, j), [chunk, chunk], 4 * half * width * step, place, dosage)
        a = exchange(a, chain, 0)
        b = exchange(b, chain, 1)
        raw.append((a, b))

    values = dosage.astype(jnp.float32)
    totals, squares = lax.psum((jnp.sum(values, 0), jnp.sum(values * values, 0)), "samp")
    mean = totals / samples
    var = squares / samples - mean * mean
    live = (jnp.arange(width, dtype=jnp.int32) < counts[0]).astype(jnp.float32)
    keep = filter_mask.astype(jnp.float32) * live
    scale = lax.rsqrt(var + 1e-05) * keep
    stats = jnp.stack([mean, scale])
    stats = jnp.concatenate([stats, spread(stats)])
    sa = exchange(stats, chain, 0)
    sb = exchange(stats, chain, 1)

    own, *parts = call(
        functools.partial(own_kernel, samp),
        [bf16(width, local_rows)] + [f32(samp // 2, part, width)] * 2,
        2 * local_rows * width * width,
        place, dosage, mean[None], scale[None],
    )
    tile = scatter_sum(*parts)

    base = call(base_kernel, [f32(width, width)] * 2, 4 * half * width * width, place, sa, sb, own, *heads)
    nears, fars, totals = [], [], []
    for j in range(chunks):
        blocks = (2 * j + 1) * share
        last = j == chunks - 1
        near, *saved, kept, sent = call(
            functools.partial(step_kernel, samp, j, not last),
            [bf16(half, step)]
            + ([] if last else [bf16(step, half)])
            + [f32(samp // 2, blocks + (0 if last else part), step)] * 2,
            2 * half * step * ((0 if last else width) + (2 * j + 1) * step),
            place, sa, sb, *raw[j], own, *base, *nears, *fars,
        )
        if not last:
            nears.append(near)
            fars += saved
            totals.append(scatter_sum(kept, sent))
    early = lax.ppermute(
        jnp.concatenate([total[part:] for total in totals]), "chain", [(i + 1, i) for i in range(chain - 2)]
    )
    kept = kept + swap(sent, 1)
    near, sent = call(
        functools.partial(near_kernel, samp, chunks - 1), [f32(samp // 2, part, step)] * 2, 2 * half * step * width,
        place, near, own, base[0],
    )
    near = near + swap(sent, 1)
    others, far = [], []
    for n in range(samp // 2):
        pairs = [((c + 1) * samp + i, c * samp + (i ^ (2 * n))) for c in range(chain - 2) for i in range(samp)]
        far.append(lax.ppermute(kept[n], ("chain", "samp"), pairs))
        if n:
            others.append(swap(near[n], 2 * n))
    (out,) = call(
        functools.partial(final_kernel, samples, chunks, share),
        [f32(3, part, width)],
        0,
        tile, near, sum(others), early, far[0], sum(far[1:]), *totals,
        scalars=False,
    )
    return jnp.swapaxes(out, 0, 1)[None]


def solution(mesh):
    in_specs = (P("samp", ("groups", "chain")), P(("groups", "chain")), P(("groups", "chain")))
    out_specs = P(("groups", "chain"), "samp", None, None)
    return jax.shard_map(body, mesh=mesh, in_specs=in_specs, out_specs=out_specs, check_vma=False)
```
